512 devices in a mesh: row: 32 (over y, x), head: 16 (over z, core).
Axes of the slice: x: 4, y: 8, z: 8, core: 2. Of those that a mesh axis runs over, the one named last changes fastest.
Arguments:
- patches: bfloat16 [196608, 768], P(('row', 'head')), may hold values from -6 to 6
- w_patch: bfloat16 [768, 1024], replicated, may hold values from -0.21875 to 0.21875
- patch_bias: float32 [1024], replicated, may hold values from -4 to 4
- w_kv: bfloat16 [1024, 2048], P(None, 'head'), may hold values from -0.1875 to 0.1875
- queries: bfloat16 [2048, 1024], P(None, 'head'), may hold values from -160 to 160
Outputs:
- readout: bfloat16 [2048, 1024], P(None, 'head')
The draws below stay inside these ranges and needn't reach their ends.
All inputs are finite; a program needn't handle non-finite values.
Results may differ from the reference program's by a relative error of at most 0.011.
Values may be sent and summed in bfloat16 or wider, within the bound.
No kernel may reach another device: no remote copies, remote signals or barrier semaphores. Data moves between devices by JAX's collectives and lax.ppermute only.
A program may use at most 128 MiB of HBM per device.

```python
import jax
import jax.numpy as jnp
from jax import lax

D = 1024
PATCH_IN = 768
HD = 64
LAT = 2048
HEADS = 16
TOKENS = 196608


def draw_queries(key, part):
    first = jax.random.fold_in(key, 0)
    base = jax.random.truncated_normal(first, -6.0, 6.0, (LAT, HEADS * HD), jnp.float32)
    return (5.0 * base).astype(jnp.bfloat16)


def levels(own_key, extent, pieces, smallest, high):
    loudness, own = 1.0, jax.random.fold_in(own_key, 6)
    for axis_at, parts in pieces:
        draws = jnp.exp(jax.random.uniform(jax.random.fold_in(own, axis_at), (parts,), jnp.float32, smallest / len(pieces), high / len(pieces)))
        loudness = loudness * jnp.repeat(draws, extent[axis_at] // parts).reshape([-1 if axis == axis_at else 1 for axis in range(len(extent))])
    return loudness


def noise(stream_key, dims, scale, limit, shards=(), dtype=jnp.bfloat16):
    loudness = levels(stream_key, dims, shards, -0.22, 0.18) if shards else 1.0
    values = jax.random.normal(stream_key, dims, jnp.float32) * scale * loudness
    return jnp.minimum(jnp.maximum(values, -limit), limit).astype(dtype)


def setup_inputs(seed: int = 0) -> dict:
    keys = jax.random.split(jax.random.key(seed), 6)
    patches = noise(keys[0], (TOKENS, PATCH_IN), 1.0, 6.0, ((0, 512),))
    w_patch = noise(keys[1], (PATCH_IN, D), PATCH_IN ** -0.5, 0.21875)
    patch_bias = noise(keys[2], (D,), 1.0, 4.0, (), jnp.float32)
    w_kv = noise(keys[3], (D, 2 * HEADS * HD), D ** -0.5, 0.1875, ((1, 16),))
    queries = draw_queries(jax.random.fold_in(keys[5], 71), 0)
    return dict(patches=patches, w_patch=w_patch, patch_bias=patch_bias, w_kv=w_kv, queries=queries)


def reference(patches, w_patch, patch_bias, w_kv, queries):
    embed = jnp.dot(patches, w_patch, preferred_element_type=jnp.float32) + patch_bias.astype(jnp.float32)
    mean = lax.optimization_barrier(jnp.mean(embed, axis=-1, keepdims=True))
    var = lax.optimization_barrier(jnp.mean((embed - mean) * (embed - mean), axis=-1, keepdims=True))
    normed = ((embed - mean) * lax.rsqrt(var + 1e-05)).astype(jnp.bfloat16)
    kv = jnp.dot(normed, w_kv, preferred_element_type=jnp.float32).astype(jnp.bfloat16)
    kv = jnp.transpose(kv.reshape(TOKENS, HEADS, 2 * HD), (1, 0, 2))
    qall = jnp.transpose(queries.reshape(LAT, HEADS, HD), (1, 0, 2))
    block = min(4096, TOKENS)
    scale = float(HD) ** (-0.5)

    def one_head(pair):
        query_head, kv_head = pair
        blocks = kv_head.reshape(TOKENS // block, block, 2 * HD)

        def step(carry, piece):
            run_max, total, accum = carry
            scores = jnp.dot(query_head, piece[:, :HD].T, preferred_element_type=jnp.float32) * scale
            new_max = jnp.maximum(run_max, lax.optimization_barrier(jnp.max(scores, axis=1)))
            factor = jnp.exp(run_max - new_max)
            probs = jnp.exp(scores - new_max[:, None])
            total = total * factor + lax.optimization_barrier(jnp.sum(probs, axis=1))
            accum = accum * factor[:, None] + jnp.dot(probs.astype(jnp.bfloat16), piece[:, HD:], preferred_element_type=jnp.float32)
            return ((new_max, total, accum), None)
        start = (jnp.full((LAT,), -jnp.inf, jnp.float32), jnp.zeros((LAT,), jnp.float32), jnp.zeros((LAT, HD), jnp.float32))
        (run_max, total, accum), _ = lax.scan(step, start, blocks)
        return accum / total[:, None]
    result = lax.map(one_head, (qall, kv))
    return jnp.transpose(result, (1, 0, 2)).reshape(LAT, HEADS * HD).astype(jnp.bfloat16)
```

```python
import functools

import jax
import jax.numpy as jnp
from jax import lax
from jax.experimental import pallas as pl
from jax.experimental.pallas import tpu as pltpu
from jax.sharding import Mesh
from jax.sharding import PartitionSpec as P

F32 = jnp.float32
BF16 = jnp.bfloat16
LOG2E = 1.4426950408889634
LIMIT = 2.0**64
CHUNKS = 1
BLOCK = 1024
ROWS = 80
PAY = 48
PLAIN = (((1,), (0,)), ((), ()))


def split(value):
    high = value.astype(BF16)
    return high, (value - high.astype(F32)).astype(BF16)


def attend_kernel(first, last, block, *refs):
    if first:
        x_ref, rstd_ref, w_ref, b_ref, q_ref = refs[:5]
        rest = refs[5:]
    else:
        x_ref, rstd_ref, w_ref, b_ref, q_ref, acc_in, m_in = refs[:7]
        rest = refs[7:]
    if last:
        pay_ref, k_ref, v_ref, qa_ref, m_ref, acc_ref = rest
    else:
        acc_ref, m_ref, k_ref, v_ref, qa_ref = rest
    tokens = x_ref.shape[0]
    heads, size, latents = q_ref.shape
    steps = tokens // block

    def at(t):
        return pl.ds(pl.multiple_of(t * block, block), block)

    def project(t, carry):
        kv = jnp.dot(x_ref[at(t), :], w_ref[...], preferred_element_type=F32)
        kv = (kv + b_ref[...]) * rstd_ref[at(t), :]
        lane = lax.broadcasted_iota(jnp.int32, (block, 2 * size), 1)
        for h in range(heads):
            mine = kv[:, 2 * size * h : 2 * size * (h + 1)]
            k_ref[h, at(t), :] = jnp.where(lane < size, mine, 1.0).astype(BF16)
            v_ref[h, t, :size, :] = mine.T[size:, :].astype(BF16)
            v_ref[h, t, size:, :] = jnp.ones((ROWS - size, block), BF16)
        return carry

    lax.fori_loop(0, steps, project, 0, unroll=2)

    def scores(h, keys):
        return lax.dot_general(k_ref[h, keys, :], qa_ref[h], PLAIN, preferred_element_type=F32)

    def set_max(h, value):
        high, low = split(value)
        m_ref[h] = high.astype(F32) + low.astype(F32)
        qa_ref[h, size : size + 16, :] = jnp.concatenate(
            [-high, -low, jnp.zeros((14, latents), BF16)], axis=0
        )

    for h in range(heads):
        qa_ref[h, :size, :] = q_ref[h]
        qa_ref[h, size:, :] = jnp.zeros((size, latents), BF16)
        if first:
            set_max(h, jnp.max(scores(h, pl.ds(0, 128)), axis=0, keepdims=True))
        else:
            set_max(h, m_in[h])

    def sweep(h):
        for t in range(steps):
            probs = jnp.exp2(scores(h, pl.ds(t * block, block))).astype(BF16)
            acc_ref[h] += lax.dot_general(v_ref[h, t], probs, PLAIN, preferred_element_type=F32)

    for h in range(heads):
        acc_ref[h] = jnp.zeros((ROWS, latents), F32) if first else acc_in[h]
        sweep(h)

        @pl.when(jnp.logical_not(jnp.max(acc_ref[h, size : size + 8, :]) < LIMIT))
        def _(h=h):
            before = m_ref[h]
            qa_ref[h, size:, :] = jnp.zeros((size, latents), BF16)

            def widen(t, best):
                return jnp.maximum(best, jnp.max(scores(h, at(t)), axis=0, keepdims=True))

            set_max(h, lax.fori_loop(0, steps, widen, before))
            if first:
                acc_ref[h] = jnp.zeros((ROWS, latents), F32)
            else:
                acc_ref[h] = acc_in[h] * jnp.exp2(before - m_ref[h])

            def redo(t, carry):
                probs = jnp.exp2(scores(h, at(t))).astype(BF16)
                acc_ref[h] += lax.dot_general(v_ref[h, t], probs, PLAIN, preferred_element_type=F32)
                return carry

            lax.fori_loop(0, steps, redo, 0)

        if last:
            for i in range(latents // 128):
                lanes = pl.ds(128 * i, 128)
                acc, total, m = acc_ref[h, :size, lanes], acc_ref[h, size : size + 1, lanes], m_ref[h, :, lanes]
                for side in range(2):
                    pay_ref[h, 2 * i + side] = pack(fold_half(acc, side), both(total, side), both(m, side))


def both(row, side):
    lane = lax.broadcasted_iota(jnp.int32, row.shape, 1)
    keep = lane < 64 if side == 0 else lane >= 64
    return jnp.where(keep, row, pltpu.roll(row, 64, 1))


def fold_half(acc, side):
    half = acc.shape[0] // 2
    low, high = acc[:half], acc[half:]
    if side == 0:
        high = pltpu.roll(high, 64, 1)
    else:
        low = pltpu.roll(low, 64, 1)
    lane = lax.broadcasted_iota(jnp.int32, low.shape, 1)
    return jnp.where(lane < 64, low, high)


def pack(acc, total, m):
    t_high, m_high = total.astype(BF16).astype(F32), m.astype(BF16).astype(F32)
    fill = jnp.zeros((PAY - acc.shape[0] - 4, acc.shape[1]), F32)
    rows = [acc, t_high, total - t_high, m_high, m - m_high, fill]
    return jnp.concatenate(rows, axis=0).astype(BF16)


def attend(x, rstd, w, b, q, state, last):
    tokens = x.shape[0]
    heads, size, latents = q.shape
    block = min(BLOCK, tokens)
    first = state is None
    vmem = pl.BlockSpec(memory_space=pltpu.VMEM)
    acc = jax.ShapeDtypeStruct((heads, ROWS, latents), F32)
    m = jax.ShapeDtypeStruct((heads, 1, latents), F32)
    scratch = [
        pltpu.VMEM((heads, tokens, 2 * size), BF16),
        pltpu.VMEM((heads, tokens // block, ROWS, block), BF16),
        pltpu.VMEM((heads, 2 * size, latents), BF16),
    ]
    if last:
        out = jax.ShapeDtypeStruct((heads, latents // 64, PAY, 128), BF16)
        scratch += [pltpu.VMEM(m.shape, F32), pltpu.VMEM(acc.shape, F32)]
    else:
        out = (acc, m)
    ins = (x, rstd, w, b, q) + (() if first else tuple(state))
    work = tokens * latents * heads
    return pl.pallas_call(
        functools.partial(attend_kernel, first, last, block),
        out_shape=out,
        in_specs=[vmem] * len(ins),
        out_specs=jax.tree.map(lambda _: vmem, out),
        scratch_shapes=scratch,
        compiler_params=pltpu.CompilerParams(vmem_limit_bytes=56 << 20),
        cost_estimate=pl.CostEstimate(
            flops=16 * work * size, bytes_accessed=x.size * 2, transcendentals=work
        ),
        name="attend",
    )(*ins)


def combine_kernel(final, parts_ref, out_ref):
    count, blocks = parts_ref.shape[:2]
    half = 32
    for j in range(blocks):
        parts = [parts_ref[i, j].astype(F32) for i in range(count)]
        ms = [p[half + 2 : half + 3] + p[half + 3 : half + 4] for p in parts]
        top = functools.reduce(jnp.maximum, ms)
        acc, total = 0.0, 0.0
        for p, m in zip(parts, ms):
            factor = jnp.exp2(m - top)
            acc = acc + p[:half] * factor
            total = total + (p[half : half + 1] + p[half + 1 : half + 2]) * factor
        out_ref[j] = (acc / total).astype(BF16) if final else pack(acc, total, top)


def combine(parts, final=False):
    vmem = pl.BlockSpec(memory_space=pltpu.VMEM)
    rows = 32 if final else PAY
    return pl.pallas_call(
        functools.partial(combine_kernel, final),
        out_shape=jax.ShapeDtypeStruct((parts.shape[1], rows, 128), BF16),
        in_specs=[vmem],
        out_specs=vmem,
        name="combine",
    )(parts)


def place_kernel(parts_ref, out_ref):
    half = parts_ref.shape[1]
    for i in range(parts_ref.shape[0] // 2):
        one, two = parts_ref[2 * i].astype(F32), parts_ref[2 * i + 1].astype(F32)
        lane = lax.broadcasted_iota(jnp.int32, one.shape, 1)
        low = jnp.where(lane < 64, one, pltpu.roll(two, 64, 1))
        high = jnp.where(lane < 64, pltpu.roll(one, 64, 1), two)
        out_ref[:half, pl.ds(128 * i, 128)] = low.astype(BF16)
        out_ref[half:, pl.ds(128 * i, 128)] = high.astype(BF16)


def place(parts):
    vmem = pl.BlockSpec(memory_space=pltpu.VMEM)
    return pl.pallas_call(
        place_kernel,
        out_shape=jax.ShapeDtypeStruct((64, 64 * parts.shape[0]), BF16),
        in_specs=[vmem],
        out_specs=vmem,
        name="place",
    )(parts)


def exchange(parts, axis):
    return lax.all_to_all(parts, axis, split_axis=0, concat_axis=0, tiled=True)


def spread(block, axis):
    return exchange(jnp.broadcast_to(block[None], (lax.axis_size(axis[0]) * lax.axis_size(axis[1]),) + block.shape), axis)


def body(patches, w_patch, patch_bias, w_kv, queries):
    size = queries.shape[1]
    latents = queries.shape[0]
    tokens = patches.shape[0]
    step = tokens // CHUNKS
    chunks = [
        lax.all_gather(patches[i * step : (i + 1) * step], "z", axis=0, tiled=True)
        for i in range(CHUNKS)
    ]

    weight = w_patch.astype(F32)
    weight = weight - jnp.mean(weight, axis=1, keepdims=True)
    bias = patch_bias - jnp.mean(patch_bias)
    embed = jnp.dot(patches, w_patch, preferred_element_type=F32) + patch_bias
    mean = jnp.mean(embed, axis=-1, keepdims=True)
    var = jnp.mean((embed - mean) * (embed - mean), axis=-1)
    rstd = lax.rsqrt(var + 1e-05)
    rstd = lax.all_gather(rstd.reshape(tokens // 128, 128), "z", axis=0, tiled=False)
    rstd = rstd.reshape(-1, CHUNKS, step)

    w_pair = lax.all_gather(w_kv, "c", axis=0, tiled=False)
    q_pair = lax.all_gather(queries.T, "c", axis=0, tiled=False)
    scale = jnp.where(jnp.arange(2 * size) < size, LOG2E * float(size) ** (-0.5), 1.0)
    fold = jnp.einsum("pd,hdn->phn", weight, w_pair.astype(F32), precision=lax.Precision.HIGHEST)
    fold = (fold * scale).reshape(weight.shape[0], -1).astype(BF16)
    fold_bias = jnp.einsum("d,hdn->hn", bias, w_pair.astype(F32), precision=lax.Precision.HIGHEST)
    fold_bias = (fold_bias * scale).reshape(1, -1)

    state = None
    for i, chunk in enumerate(chunks):
        column = rstd[:, i].reshape(-1, 1)
        state = attend(chunk, column, fold, fold_bias, q_pair, state, i == CHUNKS - 1)

    with jax.named_scope("totals"):
        part = combine(exchange(state, "c"))
        out = combine(exchange(part[:, None], ("y", "x")), final=True)
    with jax.named_scope("readout"):
        return place(spread(out[0], ("y", "x"))).T


def solution(mesh):
    grid = Mesh(mesh.devices.reshape(8, 4, 8, 2), ("y", "x", "z", "c"))
    head = P(None, ("z", "c"))
    placed = (P(("y", "x", "z", "c"), None), P(), P(), head, head)
    return jax.shard_map(body, mesh=grid, in_specs=placed, out_specs=head, check_vma=False)
```

```python
import functools

import jax
import jax.numpy as jnp
from jax import lax
from jax.experimental import pallas as pl
from jax.experimental.pallas import tpu as pltpu
from jax.sharding import Mesh
from jax.sharding import PartitionSpec as P

F32 = jnp.float32
BF16 = jnp.bfloat16
LOG2E = 1.4426950408889634
LIMIT = 2.0**64
RING = 128
BLOCK = 1024
ROWS = 80
PAY = 48
PLAIN = (((1,), (0,)), ((), ()))


def split(value):
    high = value.astype(BF16)
    return high, (value - high.astype(F32)).astype(BF16)


def attend_kernel(pieces, heads, first, last, *refs):
    xs, refs = refs[:pieces], refs[pieces:]
    rstd_ref, w_ref, b_ref, q_ref = refs[:4]
    refs = refs[4:]
    if not first:
        acc_ins, m_ins, refs = refs[:heads], refs[heads : 2 * heads], refs[2 * heads :]
    if last:
        pay_ref, refs = refs[0], refs[1:]
    acc_refs, m_refs, refs = refs[:heads], refs[heads : 2 * heads], refs[2 * heads :]
    k_ref, v_ref, qa_ref = refs
    tokens = k_ref.shape[1]
    _, size, latents = q_ref.shape
    block = min(BLOCK, tokens)
    steps = tokens // block

    def project(x, start, count):
        kv = jnp.dot(x, w_ref[...], preferred_element_type=F32)
        kv = (kv + b_ref[...]) * rstd_ref[pl.ds(start, count), :]
        lane = lax.broadcasted_iota(jnp.int32, (count, 2 * size), 1)
        for h in range(heads):
            mine = kv[:, 2 * size * h : 2 * size * (h + 1)]
            k_ref[h, pl.ds(start, count), :] = jnp.where(lane < size, mine, 1.0).astype(BF16)
            v_ref[h, :size, pl.ds(start, count)] = mine.T[size:, :].astype(BF16)

    start = 0
    for x_ref in xs:
        count = min(512, x_ref.shape[0])
        for t in range(x_ref.shape[0] // count):
            project(x_ref[pl.ds(t * count, count), :], start, count)
            start += count

    def scores(h, keys):
        return lax.dot_general(k_ref[h, keys, :], qa_ref[h], PLAIN, preferred_element_type=F32)

    def set_max(h, value):
        high, low = split(value)
        m_refs[h][...] = high.astype(F32) + low.astype(F32)
        qa_ref[h, size : size + 16, :] = jnp.concatenate(
            [-high, -low, jnp.zeros((14, latents), BF16)], axis=0
        )

    for h in range(heads):
        v_ref[h, size:, :] = jnp.ones((ROWS - size, tokens), BF16)
        qa_ref[h, :size, :] = q_ref[h]
        qa_ref[h, size:, :] = jnp.zeros((size, latents), BF16)
        if first:
            set_max(h, jnp.max(scores(h, pl.ds(0, 128)), axis=0, keepdims=True))
        else:
            set_max(h, m_ins[h][...])

    def add(h, keys):
        probs = jnp.exp2(scores(h, keys)).astype(BF16)
        acc_refs[h][...] += lax.dot_general(v_ref[h, :, keys], probs, PLAIN, preferred_element_type=F32)

    for h in range(heads):
        acc_ref, m_ref = acc_refs[h], m_refs[h]
        acc_ref[...] = jnp.zeros((ROWS, latents), F32) if first else acc_ins[h][...]
        for t in range(steps):
            add(h, pl.ds(t * block, block))

        @pl.when(jnp.logical_not(jnp.max(acc_ref[size : size + 8, :]) < LIMIT))
        def _(h=h, acc_ref=acc_ref, m_ref=m_ref):
            before = m_ref[...]
            qa_ref[h, size:, :] = jnp.zeros((size, latents), BF16)

            def at(t):
                return pl.ds(pl.multiple_of(t * block, block), block)

            def widen(t, best):
                return jnp.maximum(best, jnp.max(scores(h, at(t)), axis=0, keepdims=True))

            set_max(h, lax.fori_loop(0, steps, widen, before))
            if first:
                acc_ref[...] = jnp.zeros((ROWS, latents), F32)
            else:
                acc_ref[...] = acc_ins[h][...] * jnp.exp2(before - m_ref[...])

            def redo(t, carry):
                add(h, at(t))
                return carry

            lax.fori_loop(0, steps, redo, 0)

        if last:
            for i in range(latents // 128):
                lanes = pl.ds(128 * i, 128)
                acc, total, m = acc_ref[:size, lanes], acc_ref[size : size + 1, lanes], m_ref[:, lanes]
                for side in range(2):
                    pay_ref[2 * i + side] = pack(fold_half(acc, side), both(total, side), both(m, side))


def both(row, side):
    lane = lax.broadcasted_iota(jnp.int32, row.shape, 1)
    keep = lane < 64 if side == 0 else lane >= 64
    return jnp.where(keep, row, pltpu.roll(row, 64, 1))


def fold_half(acc, side):
    half = acc.shape[0] // 2
    low, high = acc[:half], acc[half:]
    if side == 0:
        high = pltpu.roll(high, 64, 1)
    else:
        low = pltpu.roll(low, 64, 1)
    lane = lax.broadcasted_iota(jnp.int32, low.shape, 1)
    return jnp.where(lane < 64, low, high)


def pack(acc, total, m):
    t_high, m_high = total.astype(BF16).astype(F32), m.astype(BF16).astype(F32)
    fill = jnp.zeros((PAY - acc.shape[0] - 4, acc.shape[1]), F32)
    rows = [acc, t_high, total - t_high, m_high, m - m_high, fill]
    return jnp.concatenate(rows, axis=0).astype(BF16)


def attend(xs, rstd, w, b, q, state, last):
    heads, size, latents = q.shape
    tokens = sum(x.shape[0] for x in xs)
    first = state is None
    vmem = pl.BlockSpec(memory_space=pltpu.VMEM)
    accs = [jax.ShapeDtypeStruct((ROWS, latents), F32)] * heads
    ms = [jax.ShapeDtypeStruct((1, latents), F32)] * heads
    scratch = [
        pltpu.VMEM((heads, tokens, 2 * size), BF16),
        pltpu.VMEM((heads, ROWS, tokens), BF16),
        pltpu.VMEM((heads, 2 * size, latents), BF16),
    ]
    if last:
        out = jax.ShapeDtypeStruct((latents // 64, PAY, 128), BF16)
        scratch = [pltpu.VMEM(i.shape, F32) for i in accs + ms] + scratch
    else:
        out = accs + ms
    ins = (*xs, rstd, w, b, q) + (() if first else tuple(state))
    work = tokens * latents * heads
    return pl.pallas_call(
        functools.partial(attend_kernel, len(xs), heads, first, last),
        out_shape=out,
        in_specs=[vmem] * len(ins),
        out_specs=jax.tree.map(lambda _: vmem, out),
        scratch_shapes=scratch,
        compiler_params=pltpu.CompilerParams(vmem_limit_bytes=56 << 20),
        cost_estimate=pl.CostEstimate(
            flops=16 * work * size, bytes_accessed=tokens * w.shape[0] * 2, transcendentals=work
        ),
        name="attend",
    )(*ins)


def combine_kernel(final, parts_ref, out_ref):
    count, blocks = parts_ref.shape[:2]
    half = 32
    for j in range(blocks):
        parts = [parts_ref[i, j].astype(F32) for i in range(count)]
        ms = [p[half + 2 : half + 3] + p[half + 3 : half + 4] for p in parts]
        top = functools.reduce(jnp.maximum, ms)
        acc, total = 0.0, 0.0
        for p, m in zip(parts, ms):
            factor = jnp.exp2(m - top)
            acc = acc + p[:half] * factor
            total = total + (p[half : half + 1] + p[half + 1 : half + 2]) * factor
        out_ref[j] = (acc / total).astype(BF16) if final else pack(acc, total, top)


def combine(parts, final=False):
    vmem = pl.BlockSpec(memory_space=pltpu.VMEM)
    rows = 32 if final else PAY
    return pl.pallas_call(
        functools.partial(combine_kernel, final),
        out_shape=jax.ShapeDtypeStruct((parts.shape[1], rows, 128), BF16),
        in_specs=[vmem],
        out_specs=vmem,
        name="combine",
    )(parts)


def place_kernel(parts_ref, out_ref):
    half = parts_ref.shape[1]
    for i in range(parts_ref.shape[0] // 2):
        one, two = parts_ref[2 * i].astype(F32), parts_ref[2 * i + 1].astype(F32)
        lane = lax.broadcasted_iota(jnp.int32, one.shape, 1)
        low = jnp.where(lane < 64, one, pltpu.roll(two, 64, 1))
        high = jnp.where(lane < 64, pltpu.roll(one, 64, 1), two)
        out_ref[:half, pl.ds(128 * i, 128)] = low.astype(BF16)
        out_ref[half:, pl.ds(128 * i, 128)] = high.astype(BF16)


def place(parts):
    vmem = pl.BlockSpec(memory_space=pltpu.VMEM)
    return pl.pallas_call(
        place_kernel,
        out_shape=jax.ShapeDtypeStruct((64, 64 * parts.shape[0]), BF16),
        in_specs=[vmem],
        out_specs=vmem,
        name="place",
    )(parts)


def exchange(parts, axis):
    return lax.all_to_all(parts, axis, split_axis=0, concat_axis=0, tiled=True)


def spread(block, axis):
    return exchange(jnp.broadcast_to(block[None], (lax.axis_size(axis[0]) * lax.axis_size(axis[1]),) + block.shape), axis)


def shift(block, axis, by):
    size = lax.axis_size(axis)
    return lax.ppermute(block, axis, [(i, (i + by) % size) for i in range(size)])


def ring(block):
    half = block.shape[0] // 2
    blocks, up, down = [block], block, block
    for _ in range(3):
        up, down = shift(up, "z", 1), shift(down, "z", -1)
        blocks += [up, down]
    last = [shift(up[:half], "z", 1), shift(down[half:], "z", -1)]
    return blocks + [jnp.concatenate(last, axis=0)]


def body(patches, w_patch, patch_bias, w_kv, queries):
    size = queries.shape[1]
    tokens = patches.shape[0]
    rest = lax.all_gather(patches[RING:], "z", axis=0, tiled=True)
    blocks = ring(patches[:RING])

    weight = w_patch.astype(F32)
    weight = weight - jnp.mean(weight, axis=1, keepdims=True)
    bias = patch_bias - jnp.mean(patch_bias)
    embed = jnp.dot(patches, w_patch, preferred_element_type=F32) + patch_bias
    mean = jnp.mean(embed, axis=-1, keepdims=True)
    var = jnp.mean((embed - mean) * (embed - mean), axis=-1)
    rstd = lax.rsqrt(var + 1e-05)
    rstd = lax.all_gather(rstd.reshape(tokens // 128, 128), "z", axis=0, tiled=False)
    rstd = rstd.reshape(-1, tokens)
    turned = jnp.concatenate([rstd, rstd])[:, :RING]
    turned = lax.dynamic_slice_in_dim(turned, lax.axis_index("z"), 8, axis=0)
    order = [0, 7, 1, 6, 2, 5, 3, 4]
    rstd_ring = jnp.concatenate([turned[i : i + 1] for i in order]).reshape(-1, 1)
    rstd_rest = rstd[:, RING:].reshape(-1, 1)

    w_pair = jnp.stack([shift(w_kv, "c", 1), w_kv])
    q_pair = jnp.stack([shift(queries.T, "c", 1), queries.T])
    scale = jnp.where(jnp.arange(2 * size) < size, LOG2E * float(size) ** (-0.5), 1.0)
    fold = jnp.einsum("pd,hdn->hpn", weight, w_pair.astype(F32), precision=lax.Precision.HIGHEST)
    fold = (fold * scale).astype(BF16)
    fold_bias = jnp.einsum("d,hdn->hn", bias, w_pair.astype(F32), precision=lax.Precision.HIGHEST)
    fold_bias = fold_bias * scale

    state = attend(
        blocks, rstd_ring, jnp.concatenate([fold[0], fold[1]], axis=1),
        fold_bias.reshape(1, -1), q_pair, None, False,
    )
    pays = [
        attend(
            [rest], rstd_rest, fold[h], fold_bias[h][None], q_pair[h : h + 1],
            (state[h], state[2 + h]), True,
        )
        for h in range(2)
    ]

    with jax.named_scope("totals"):
        part = combine(jnp.stack([shift(pays[0], "c", 1), pays[1]]))
        out = combine(exchange(part[:, None], ("y", "x")), final=True)
    with jax.named_scope("readout"):
        return place(spread(out[0], ("y", "x"))).T


def solution(mesh):
    grid = Mesh(mesh.devices.reshape(8, 4, 8, 2), ("y", "x", "z", "c"))
    head = P(None, ("z", "c"))
    placed = (P(("y", "x", "z", "c"), None), P(), P(), head, head)
    return jax.shard_map(body, mesh=grid, in_specs=placed, out_specs=head, check_vma=False)
```

```python
import functools

import jax
import jax.numpy as jnp
from jax import lax
from jax.experimental import pallas as pl
from jax.experimental.pallas import tpu as pltpu
from jax.sharding import Mesh
from jax.sharding import PartitionSpec as P

F32 = jnp.float32
BF16 = jnp.bfloat16
LOG2E = 1.4426950408889634
LIMIT = 2.0**64
RING = 128
BLOCK = 1024
ROWS = 80
PAY = 48
PLAIN = (((1,), (0,)), ((), ()))


def split(value):
    high = value.astype(BF16)
    return high, (value - high.astype(F32)).astype(BF16)


def attend_kernel(mode, pieces, *refs):
    if mode != "end":
        xs, (rstd_ref, w_ref, b_ref), refs = refs[:pieces], refs[pieces : pieces + 3], refs[pieces + 3 :]
    else:
        (k_ref, v_ref), refs = refs[:2], refs[2:]
    q_ref, refs = refs[0], refs[1:]
    heads, size, latents = q_ref.shape
    if mode != "first":
        acc_ins, m_ins, refs = refs[:heads], refs[heads : 2 * heads], refs[2 * heads :]
        pay_ref, refs = refs[0], refs[1:]
    if mode == "mid":
        (k_out, v_out), refs = refs[:2], refs[2:]
    acc_refs, m_refs, refs = refs[:heads], refs[heads : 2 * heads], refs[2 * heads :]
    qa_ref, refs = refs[0], refs[1:]
    if mode != "end":
        (k_ref, v_ref), refs = refs[:2], refs[2:]
    tokens = k_ref.shape[1]
    block = min(BLOCK, tokens)
    steps = tokens // block
    keys_of = [k_ref.at[0], k_out.at[0]] if mode == "mid" else [k_ref.at[h] for h in range(heads)]
    values_of = [v_ref.at[0], v_out.at[0]] if mode == "mid" else [v_ref.at[h] for h in range(heads)]

    def project(x, start, count):
        kv = jnp.dot(x, w_ref[...], preferred_element_type=F32)
        kv = (kv + b_ref[...]) * rstd_ref[pl.ds(start, count), :]
        lane = lax.broadcasted_iota(jnp.int32, (count, 2 * size), 1)
        for h in range(2):
            mine = kv[:, 2 * size * h : 2 * size * (h + 1)]
            keys_of[h][pl.ds(start, count), :] = jnp.where(lane < size, mine, 1.0).astype(BF16)
            values_of[h][:size, pl.ds(start, count)] = mine.T[size:, :].astype(BF16)

    if mode == "first":
        start = 0
        for x_ref in xs:
            count = x_ref.shape[0]
            project(x_ref[...], start, count)
            start += count
    if mode == "mid":
        x_buf, sems = refs
        count = tokens // 4
        copies = [
            pltpu.make_async_copy(xs[0].at[pl.ds(t * count, count)], x_buf.at[t], sems.at[t])
            for t in range(4)
        ]
        for copy in copies:
            copy.start()
        for t in range(4):
            copies[t].wait()
            project(x_buf[t], t * count, count)
    if mode != "end":
        for h in range(2):
            values_of[h][size:, :] = jnp.ones((ROWS - size, tokens), BF16)

    def scores(h, keys):
        return lax.dot_general(keys_of[h][keys, :], qa_ref[h], PLAIN, preferred_element_type=F32)

    def set_max(h, value):
        high, low = split(value)
        m_refs[h][...] = high.astype(F32) + low.astype(F32)
        qa_ref[h, size : size + 16, :] = jnp.concatenate(
            [-high, -low, jnp.zeros((14, latents), BF16)], axis=0
        )

    for h in range(heads):
        qa_ref[h, :size, :] = q_ref[h]
        qa_ref[h, size:, :] = jnp.zeros((size, latents), BF16)
        if mode == "first":
            set_max(h, jnp.max(scores(h, pl.ds(0, 128)), axis=0, keepdims=True))
        else:
            set_max(h, m_ins[h][...])

    def add(h, keys):
        probs = jnp.exp2(scores(h, keys)).astype(BF16)
        return lax.dot_general(values_of[h][:, keys], probs, PLAIN, preferred_element_type=F32)

    for h in range(heads):
        acc_ref, m_ref = acc_refs[h], m_refs[h]
        for t in range(steps):
            more = add(h, pl.ds(t * block, block))
            if t > 0:
                acc_ref[...] += more
            else:
                acc_ref[...] = more if mode == "first" else acc_ins[h][...] + more

        @pl.when(jnp.logical_not(jnp.max(acc_ref[size : size + 8, :]) < LIMIT))
        def _(h=h, acc_ref=acc_ref, m_ref=m_ref):
            before = m_ref[...]
            qa_ref[h, size:, :] = jnp.zeros((size, latents), BF16)

            def at(t):
                return pl.ds(pl.multiple_of(t * block, block), block)

            def widen(t, best):
                return jnp.maximum(best, jnp.max(scores(h, at(t)), axis=0, keepdims=True))

            set_max(h, lax.fori_loop(0, steps, widen, before))
            if mode == "first":
                acc_ref[...] = jnp.zeros((ROWS, latents), F32)
            else:
                acc_ref[...] = acc_ins[h][...] * jnp.exp2(before - m_ref[...])

            def redo(t, carry):
                acc_ref[...] += add(h, at(t))
                return carry

            lax.fori_loop(0, steps, redo, 0)

        if mode != "first":
            for i in range(latents // 128):
                lanes = pl.ds(128 * i, 128)
                acc, total, m = acc_ref[:size, lanes], acc_ref[size : size + 1, lanes], m_ref[:, lanes]
                for side in range(2):
                    pay_ref[2 * i + side] = pack(fold_half(acc, side), both(total, side), both(m, side))


def both(row, side):
    lane = lax.broadcasted_iota(jnp.int32, row.shape, 1)
    keep = lane < 64 if side == 0 else lane >= 64
    return jnp.where(keep, row, pltpu.roll(row, 64, 1))


def fold_half(acc, side):
    half = acc.shape[0] // 2
    low, high = acc[:half], acc[half:]
    if side == 0:
        high = pltpu.roll(high, 64, 1)
    else:
        low = pltpu.roll(low, 64, 1)
    lane = lax.broadcasted_iota(jnp.int32, low.shape, 1)
    return jnp.where(lane < 64, low, high)


def pack(acc, total, m):
    t_high, m_high = total.astype(BF16).astype(F32), m.astype(BF16).astype(F32)
    fill = jnp.zeros((PAY - acc.shape[0] - 4, acc.shape[1]), F32)
    rows = [acc, t_high, total - t_high, m_high, m - m_high, fill]
    return jnp.concatenate(rows, axis=0).astype(BF16)


def attend(mode, source, q, state=()):
    heads, size, latents = q.shape
    vmem = pl.BlockSpec(memory_space=pltpu.VMEM)
    pieces = len(source) - 3
    tokens = source[0].shape[1] if mode == "end" else sum(x.shape[0] for x in source[:pieces])
    accs = [jax.ShapeDtypeStruct((ROWS, latents), F32)] * heads
    ms = [jax.ShapeDtypeStruct((1, latents), F32)] * heads
    keys = jax.ShapeDtypeStruct((heads, tokens, 2 * size), BF16)
    values = jax.ShapeDtypeStruct((heads, ROWS, tokens), BF16)
    pay = jax.ShapeDtypeStruct((latents // 64, PAY, 128), BF16)
    ins = (*source, q, *state)
    in_specs = [vmem] * len(ins)
    scratch = [pltpu.VMEM((heads, 2 * size, latents), BF16)]
    if mode != "end":
        scratch += [pltpu.VMEM(keys.shape, BF16), pltpu.VMEM(values.shape, BF16)]
    out = accs + ms
    if mode != "first":
        scratch = [pltpu.VMEM(i.shape, F32) for i in accs + ms] + scratch
        out = [pay]
    if mode == "mid":
        out = [pay, keys, values]
        in_specs[0] = pl.BlockSpec(memory_space=pl.ANY)
        scratch += [
            pltpu.VMEM((4, tokens // 4, source[0].shape[1]), BF16),
            pltpu.SemaphoreType.DMA((4,)),
        ]
    work = tokens * latents * heads
    return pl.pallas_call(
        functools.partial(attend_kernel, mode, pieces),
        out_shape=out,
        in_specs=in_specs,
        out_specs=[vmem] * len(out),
        scratch_shapes=scratch,
        compiler_params=pltpu.CompilerParams(vmem_limit_bytes=56 << 20),
        cost_estimate=pl.CostEstimate(
            flops=16 * work * size, bytes_accessed=tokens * 1536, transcendentals=work
        ),
        name="attend",
    )(*ins)


def merge(parts):
    half = 32
    ms = [p[half + 2 : half + 3] + p[half + 3 : half + 4] for p in parts]
    top = functools.reduce(jnp.maximum, ms)
    acc, total = 0.0, 0.0
    for p, m in zip(parts, ms):
        factor = jnp.exp2(m - top)
        acc = acc + p[:half] * factor
        total = total + (p[half : half + 1] + p[half + 1 : half + 2]) * factor
    return acc, total, top


def combine_kernel(one_ref, two_ref, out_ref):
    for j in range(one_ref.shape[0]):
        out_ref[j] = pack(*merge([one_ref[j].astype(F32), two_ref[j].astype(F32)]))


def finish_kernel(parts_ref, out_ref):
    acc, total, _ = merge([parts_ref[i].astype(F32) for i in range(parts_ref.shape[0])])
    result = (acc / total).astype(BF16)
    for i in range(out_ref.shape[0]):
        out_ref[i] = result


def combine(one, two):
    vmem = pl.BlockSpec(memory_space=pltpu.VMEM)
    return pl.pallas_call(
        combine_kernel,
        out_shape=jax.ShapeDtypeStruct(one.shape, BF16),
        in_specs=[vmem] * 2,
        out_specs=vmem,
        name="combine",
    )(one, two)


def finish(parts):
    vmem = pl.BlockSpec(memory_space=pltpu.VMEM)
    return pl.pallas_call(
        finish_kernel,
        out_shape=jax.ShapeDtypeStruct((parts.shape[0], 32, 128), BF16),
        in_specs=[vmem],
        out_specs=vmem,
        name="finish",
    )(parts)


def place_kernel(parts_ref, out_ref):
    half = parts_ref.shape[1]
    for i in range(parts_ref.shape[0] // 2):
        one, two = parts_ref[2 * i].astype(F32), parts_ref[2 * i + 1].astype(F32)
        lane = lax.broadcasted_iota(jnp.int32, one.shape, 1)
        low = jnp.where(lane < 64, one, pltpu.roll(two, 64, 1))
        high = jnp.where(lane < 64, pltpu.roll(one, 64, 1), two)
        out_ref[:half, pl.ds(128 * i, 128)] = low.astype(BF16)
        out_ref[half:, pl.ds(128 * i, 128)] = high.astype(BF16)


def place(parts):
    vmem = pl.BlockSpec(memory_space=pltpu.VMEM)
    return pl.pallas_call(
        place_kernel,
        out_shape=jax.ShapeDtypeStruct((64, 64 * parts.shape[0]), BF16),
        in_specs=[vmem],
        out_specs=vmem,
        name="place",
    )(parts)


def exchange(parts, axis):
    return lax.all_to_all(parts, axis, split_axis=0, concat_axis=0, tiled=True)


def shift(block, axis, by):
    size = lax.axis_size(axis)
    return lax.ppermute(block, axis, [(i, (i + by) % size) for i in range(size)])


def ring(block):
    half = block.shape[0] // 2
    blocks, up, down = [block], block, block
    for _ in range(3):
        up, down = shift(up, "z", 1), shift(down, "z", -1)
        blocks += [up, down]
    last = [shift(up[:half], "z", 1), shift(down[half:], "z", -1)]
    return blocks + [jnp.concatenate(last, axis=0)]


def body(patches, w_patch, patch_bias, w_kv, queries):
    size = queries.shape[1]
    tokens = patches.shape[0]
    rest = lax.all_gather(patches[RING:], "z", axis=0, tiled=True)
    blocks = ring(patches[:RING])

    weight = w_patch.astype(F32)
    weight = weight - jnp.mean(weight, axis=1, keepdims=True)
    bias = patch_bias - jnp.mean(patch_bias)
    embed = jnp.dot(patches, w_patch, preferred_element_type=F32) + patch_bias
    mean = jnp.mean(embed, axis=-1, keepdims=True)
    var = jnp.mean((embed - mean) * (embed - mean), axis=-1)
    rstd = lax.rsqrt(var + 1e-05)
    rstd = exchange(jnp.broadcast_to(rstd[None], (lax.axis_size("z"), tokens)), "z")
    turned = jnp.concatenate([rstd, rstd])[:, :RING]
    turned = lax.dynamic_slice_in_dim(turned, lax.axis_index("z"), 8, axis=0)
    order = [0, 7, 1, 6, 2, 5, 3, 4]
    rstd_ring = jnp.concatenate([turned[i : i + 1] for i in order]).reshape(-1, 1)
    rstd_rest = rstd[:, RING:].reshape(-1, 1)

    w_pair = jnp.stack([shift(w_kv, "c", 1), w_kv])
    q_pair = jnp.stack([shift(queries.T, "c", 1), queries.T])
    scale = jnp.where(jnp.arange(2 * size) < size, LOG2E * float(size) ** (-0.5), 1.0)
    fold = jnp.einsum("pd,hdn->hpn", weight, w_pair.astype(F32), precision=lax.Precision.HIGHEST)
    fold = (fold * scale).astype(BF16)
    fold_bias = jnp.einsum("d,hdn->hn", bias, w_pair.astype(F32), precision=lax.Precision.HIGHEST)
    fold_bias = fold_bias * scale

    both_heads = (jnp.concatenate([fold[0], fold[1]], axis=1), fold_bias.reshape(1, -1))
    state = attend("first", (*blocks, rstd_ring, *both_heads), q_pair)
    other, keys, values = attend(
        "mid", (rest, rstd_rest, *both_heads), q_pair[:1], (state[0], state[2])
    )
    arrived = shift(other, "c", 1)
    (own,) = attend("end", (keys, values), q_pair[1:], (state[1], state[3]))

    with jax.named_scope("totals"):
        part = finish(exchange(combine(own, arrived), ("y", "x")))
    with jax.named_scope("readout"):
        return place(exchange(part, ("y", "x"))).T


def solution(mesh):
    grid = Mesh(mesh.devices.reshape(8, 4, 8, 2), ("y", "x", "z", "c"))
    head = P(None, ("z", "c"))
    placed = (P(("y", "x", "z", "c"), None), P(), P(), head, head)
    return jax.shard_map(body, mesh=grid, in_specs=placed, out_specs=head, check_vma=False)
```

```python
import functools

import jax
import jax.numpy as jnp
from jax import lax
from jax.experimental import pallas as pl
from jax.experimental.pallas import tpu as pltpu
from jax.sharding import Mesh
from jax.sharding import PartitionSpec as P

F32 = jnp.float32
BF16 = jnp.bfloat16
LOG2E = 1.4426950408889634
LIMIT = 2.0**64
ROWS = 80
BLOCK = 1024
PAY = 48
PLAIN = (((1,), (0,)), ((), ()))


def split(value):
    high = value.astype(BF16)
    return high, (value - high.astype(F32)).astype(BF16)


def attend_kernel(first, *refs):
    if first:
        x_ref, rstd_ref, w_ref, b_ref, q_ref, *refs = refs
        acc_refs, m_refs, (qa_ref, k_ref, v_ref) = refs[:2], refs[2:4], refs[4:]
    else:
        at_ref, x_ref, rstd_ref, w_ref, b_ref, q_ref, *refs = refs
        acc_ins, m_ins, pay_refs, refs = refs[:2], refs[2:4], refs[4:6], refs[6:]
        acc_refs, m_refs, (qa_ref, k_ref, v_ref, x_buf, sems) = refs[:2], refs[2:4], refs[4:]
    tokens = k_ref.shape[1]
    heads, size, latents = q_ref.shape
    block = 128
    steps = tokens // block

    def project(x, start, count):
        kv = jnp.dot(x, w_ref[...], preferred_element_type=F32)
        kv = (kv + b_ref[...]) * rstd_ref[pl.ds(start, count), :]
        lane = lax.broadcasted_iota(jnp.int32, (count, 2 * size), 1)
        for h in range(heads):
            mine = kv[:, 2 * size * h : 2 * size * (h + 1)].astype(BF16)
            k_ref[h, pl.ds(start, count), :] = jnp.where(lane < size, mine, jnp.ones_like(mine))
            v_ref[h, :size, pl.ds(start, count)] = mine.T[size:, :]

    for h in range(heads):
        v_ref[h, size:, :] = jnp.ones((ROWS - size, tokens), BF16)
        qa_ref[h, :size, :] = q_ref[h]
        qa_ref[h, size:, :] = jnp.zeros((size, latents), BF16)

    if first:
        project(x_ref[...], 0, tokens)
    else:
        pieces, count = x_buf.shape[:2]
        copies = []
        for t in range(pieces):
            place = lax.rem(at_ref[0] + t + 1, pieces + 1)
            rows = pl.ds(pl.multiple_of(place * count, count), count)
            copies.append(pltpu.make_async_copy(x_ref.at[rows], x_buf.at[t], sems.at[t]))
            copies[t].start()
        for t in range(pieces):
            copies[t].wait()
            project(x_buf[t], t * count, count)

    def scores(h, keys):
        return lax.dot_general(k_ref[h, keys, :], qa_ref[h], PLAIN, preferred_element_type=F32)

    def set_max(h, value):
        high, low = split(value)
        m_refs[h][...] = high.astype(F32) + low.astype(F32)
        qa_ref[h, size : size + 16, :] = jnp.concatenate(
            [-high, -low, jnp.zeros((14, latents), BF16)], axis=0
        )

    for h in range(heads):
        if first:
            set_max(h, jnp.max(scores(h, pl.ds(0, 128)), axis=0, keepdims=True))
        else:
            set_max(h, m_ins[h][...])

    def add(h, keys):
        probs = jnp.exp2(scores(h, keys)).astype(BF16)
        return lax.dot_general(v_ref[h, :, keys], probs, PLAIN, preferred_element_type=F32)

    for h in range(heads):
        acc_ref, m_ref = acc_refs[h], m_refs[h]
        for t in range(0, tokens, BLOCK):
            more = add(h, pl.ds(t, min(BLOCK, tokens - t)))
            if t > 0:
                acc_ref[...] += more
            else:
                acc_ref[...] = more if first else acc_ins[h][...] + more

        @pl.when(jnp.logical_not(jnp.max(acc_ref[size : size + 8, :]) < LIMIT))
        def _(h=h, acc_ref=acc_ref, m_ref=m_ref):
            before = m_ref[...]
            qa_ref[h, size:, :] = jnp.zeros((size, latents), BF16)

            def at(t):
                return pl.ds(pl.multiple_of(t * block, block), block)

            def widen(t, best):
                return jnp.maximum(best, jnp.max(scores(h, at(t)), axis=0, keepdims=True))

            set_max(h, lax.fori_loop(0, steps, widen, before))
            if first:
                acc_ref[...] = jnp.zeros((ROWS, latents), F32)
            else:
                acc_ref[...] = acc_ins[h][...] * jnp.exp2(before - m_ref[...])

            def redo(t, carry):
                acc_ref[...] += add(h, at(t))
                return carry

            lax.fori_loop(0, steps, redo, 0)

        if not first:
            for i in range(latents // 128):
                lanes = pl.ds(128 * i, 128)
                acc, total, m = acc_ref[:size, lanes], acc_ref[size : size + 1, lanes], m_ref[:, lanes]
                for side in range(2):
                    pay_refs[h][2 * i + side] = pack(fold_half(acc, side), both(total, side), both(m, side))


def both(row, side):
    lane = lax.broadcasted_iota(jnp.int32, row.shape, 1)
    keep = lane < 64 if side == 0 else lane >= 64
    return jnp.where(keep, row, pltpu.roll(row, 64, 1))


def fold_half(acc, side):
    half = acc.shape[0] // 2
    low, high = acc[:half], acc[half:]
    if side == 0:
        high = pltpu.roll(high, 64, 1)
    else:
        low = pltpu.roll(low, 64, 1)
    lane = lax.broadcasted_iota(jnp.int32, low.shape, 1)
    return jnp.where(lane < 64, low, high)


def pack(acc, total, m):
    t_high, m_high = total.astype(BF16).astype(F32), m.astype(BF16).astype(F32)
    fill = jnp.zeros((PAY - acc.shape[0] - 4, acc.shape[1]), F32)
    rows = [acc, t_high, total - t_high, m_high, m - m_high, fill]
    return jnp.concatenate(rows, axis=0).astype(BF16)


def attend(x, rstd, w, b, q, at=None, state=()):
    heads, size, latents = q.shape
    first = at is None
    vmem = pl.BlockSpec(memory_space=pltpu.VMEM)
    tokens = rstd.shape[0]
    accs = [jax.ShapeDtypeStruct((ROWS, latents), F32)] * heads
    ms = [jax.ShapeDtypeStruct((1, latents), F32)] * heads
    scratch = [
        pltpu.VMEM((heads, 2 * size, latents), BF16),
        pltpu.VMEM((heads, tokens, 2 * size), BF16),
        pltpu.VMEM((heads, ROWS, tokens), BF16),
    ]
    if first:
        ins, in_specs, out = (x, rstd, w, b, q), [vmem] * 5, accs + ms
    else:
        count = x.shape[0] - tokens
        ins = (at, x, rstd, w, b, q, *state)
        in_specs = [pl.BlockSpec(memory_space=pltpu.SMEM), pl.BlockSpec(memory_space=pl.ANY)]
        in_specs += [vmem] * (len(ins) - 2)
        out = [jax.ShapeDtypeStruct((latents // 64, PAY, 128), BF16)] * heads
        scratch = [pltpu.VMEM(i.shape, F32) for i in accs + ms] + scratch
        scratch += [
            pltpu.VMEM((tokens // count, count, x.shape[1]), BF16),
            pltpu.SemaphoreType.DMA((tokens // count,)),
        ]
    work = tokens * latents * heads
    return pl.pallas_call(
        functools.partial(attend_kernel, first),
        out_shape=out,
        in_specs=in_specs,
        out_specs=[vmem] * len(out),
        scratch_shapes=scratch,
        compiler_params=pltpu.CompilerParams(vmem_limit_bytes=56 << 20),
        cost_estimate=pl.CostEstimate(
            flops=16 * work * size, bytes_accessed=tokens * 1536, transcendentals=work
        ),
        name="attend",
    )(*ins)


def merge(parts):
    half = 32
    ms = [p[half + 2 : half + 3] + p[half + 3 : half + 4] for p in parts]
    top = functools.reduce(jnp.maximum, ms)
    acc, total = 0.0, 0.0
    for p, m in zip(parts, ms):
        factor = jnp.exp2(m - top)
        acc = acc + p[:half] * factor
        total = total + (p[half : half + 1] + p[half + 1 : half + 2]) * factor
    return acc, total, top


def combine_kernel(one_ref, two_ref, out_ref):
    for j in range(one_ref.shape[0]):
        out_ref[j] = pack(*merge([one_ref[j].astype(F32), two_ref[j].astype(F32)]))


def finish_kernel(last, parts_ref, out_ref):
    for j in range(parts_ref.shape[1]):
        merged = merge([parts_ref[i, j].astype(F32) for i in range(parts_ref.shape[0])])
        result = (merged[0] / merged[1]).astype(BF16) if last else pack(*merged)
        for i in range(out_ref.shape[0]):
            out_ref[i, j] = result


def combine(one, two):
    vmem = pl.BlockSpec(memory_space=pltpu.VMEM)
    return pl.pallas_call(
        combine_kernel,
        out_shape=jax.ShapeDtypeStruct(one.shape, BF16),
        in_specs=[vmem] * 2,
        out_specs=vmem,
        name="combine",
    )(one, two)


def finish(parts, copies, last):
    vmem = pl.BlockSpec(memory_space=pltpu.VMEM)
    return pl.pallas_call(
        functools.partial(finish_kernel, last),
        out_shape=jax.ShapeDtypeStruct((copies, parts.shape[1], 32 if last else PAY, 128), BF16),
        in_specs=[vmem],
        out_specs=vmem,
        name="finish",
    )(parts)


def place_kernel(parts_ref, out_ref):
    half = parts_ref.shape[1]
    for i in range(parts_ref.shape[0] // 2):
        one, two = parts_ref[2 * i].astype(F32), parts_ref[2 * i + 1].astype(F32)
        lane = lax.broadcasted_iota(jnp.int32, one.shape, 1)
        low = jnp.where(lane < 64, one, pltpu.roll(two, 64, 1))
        high = jnp.where(lane < 64, pltpu.roll(one, 64, 1), two)
        out_ref[:half, pl.ds(128 * i, 128)] = low.astype(BF16)
        out_ref[half:, pl.ds(128 * i, 128)] = high.astype(BF16)


def place(parts):
    vmem = pl.BlockSpec(memory_space=pltpu.VMEM)
    return pl.pallas_call(
        place_kernel,
        out_shape=jax.ShapeDtypeStruct((64, 64 * parts.shape[0]), BF16),
        in_specs=[vmem],
        out_specs=vmem,
        name="place",
    )(parts)


def exchange(parts, axis):
    return lax.all_to_all(parts, axis, split_axis=0, concat_axis=0, tiled=True)


def shift(block, axis, by):
    size = lax.axis_size(axis)
    return lax.ppermute(block, axis, [(i, (i + by) % size) for i in range(size)])


def body(patches, w_patch, patch_bias, w_kv, queries):
    size = queries.shape[1]
    tokens = patches.shape[0]
    gathered = lax.all_gather(patches, "z", axis=0, tiled=True)

    weight = w_patch.astype(F32)
    weight = weight - jnp.mean(weight, axis=1, keepdims=True)
    bias = patch_bias - jnp.mean(patch_bias)
    embed = jnp.dot(patches, w_patch, preferred_element_type=F32) + patch_bias
    mean = jnp.mean(embed, axis=-1, keepdims=True)
    var = jnp.mean((embed - mean) * (embed - mean), axis=-1)
    rstd = lax.rsqrt(var + 1e-05)
    mine = rstd.reshape(-1, 1)
    rstd = exchange(jnp.broadcast_to(rstd[None], (lax.axis_size("z"), tokens)), "z")
    at = lax.axis_index("z")
    turned = lax.dynamic_slice_in_dim(jnp.concatenate([rstd, rstd]), at + 1, rstd.shape[0] - 1, axis=0)

    w_pair = jnp.stack([shift(w_kv, "c", 1), w_kv])
    q_pair = jnp.stack([shift(queries.T, "c", 1), queries.T])
    scale = jnp.where(jnp.arange(2 * size) < size, LOG2E * float(size) ** (-0.5), 1.0)
    fold = jnp.einsum("pd,hdn->hpn", weight, w_pair.astype(F32), precision=lax.Precision.HIGHEST)
    fold = (fold * scale).astype(BF16)
    fold_bias = jnp.einsum("d,hdn->hn", bias, w_pair.astype(F32), precision=lax.Precision.HIGHEST)
    fold_bias = fold_bias * scale

    weights = (jnp.concatenate([fold[0], fold[1]], axis=1), fold_bias.reshape(1, -1), q_pair)
    state = attend(patches, mine, *weights)
    other, own = attend(gathered, turned.reshape(-1, 1), *weights, at.reshape(1), state)

    with jax.named_scope("totals"):
        part = combine(own, shift(other, "c", 1))
        part = exchange(part.reshape(lax.axis_size("y"), -1, PAY, 128), "y")
        part = exchange(finish(part, lax.axis_size("x"), False), "x")
    with jax.named_scope("readout"):
        part = exchange(finish(part, lax.axis_size("y"), True), "y")
        return place(part.reshape(-1, 32, 128)).T


def solution(mesh):
    grid = Mesh(mesh.devices.reshape(8, 4, 8, 2), ("y", "x", "z", "c"))
    head = P(None, ("z", "c"))
    placed = (P(("y", "x", "z", "c"), None), P(), P(), head, head)
    return jax.shard_map(body, mesh=grid, in_specs=placed, out_specs=head, check_vma=False)
```

```python
import functools

import jax
import jax.numpy as jnp
from jax import lax
from jax.experimental import pallas as pl
from jax.experimental.pallas import tpu as pltpu
from jax.sharding import Mesh
from jax.sharding import PartitionSpec as P

F32 = jnp.float32
BF16 = jnp.bfloat16
LOG2E = 1.4426950408889634
LIMIT = 2.0**64
ROWS = 80
BLOCK = 1024
PAY = 40
PLAIN = (((1,), (0,)), ((), ()))


def split(value):
    high = value.astype(BF16)
    return high, (value - high.astype(F32)).astype(BF16)


def attend_kernel(first, *refs):
    if first:
        x_ref, rstd_ref, w_ref, b_ref, q_ref, *refs = refs
        acc_refs, m_refs, (qa_ref, k_ref, v_ref) = refs[:2], refs[2:4], refs[4:]
    else:
        at_ref, x_ref, rstd_ref, w_ref, b_ref, q_ref, *refs = refs
        acc_ins, m_ins, pay_refs, refs = refs[:2], refs[2:4], refs[4:6], refs[6:]
        acc_refs, m_refs, (qa_ref, k_ref, v_ref, x_buf, sems) = refs[:2], refs[2:4], refs[4:]
    tokens = k_ref.shape[1]
    heads, size, latents = q_ref.shape
    block = 128
    steps = tokens // block

    if not first:
        pieces, count = x_buf.shape[:2]
        copies = []
        for t in range(pieces):
            place = lax.rem(at_ref[0] + t + 1, pieces + 1)
            rows = pl.ds(pl.multiple_of(place * count, count), count)
            copies.append(pltpu.make_async_copy(x_ref.at[rows], x_buf.at[t], sems.at[t]))
            copies[t].start()

    def project(x, start, count):
        kv = jnp.dot(x, w_ref[...], preferred_element_type=F32)
        kv = (kv + b_ref[...]) * rstd_ref[pl.ds(start, count), :]
        lane = lax.broadcasted_iota(jnp.int32, (count, 2 * size), 1)
        for h in range(heads):
            mine = kv[:, 2 * size * h : 2 * size * (h + 1)].astype(BF16)
            k_ref[h, pl.ds(start, count), :] = jnp.where(lane < size, mine, jnp.ones_like(mine))
            v_ref[h, :size, pl.ds(start, count)] = mine.T[size:, :]

    for h in range(heads):
        v_ref[h, size:, :] = jnp.ones((ROWS - size, tokens), BF16)
        qa_ref[h, :size, :] = q_ref[h]
        qa_ref[h, size:, :] = jnp.zeros((size, latents), BF16)

    if first:
        project(x_ref[...], 0, tokens)
    else:
        for t in range(pieces):
            copies[t].wait()
            project(x_buf[t], t * count, count)

    def scores(h, keys):
        return lax.dot_general(k_ref[h, keys, :], qa_ref[h], PLAIN, preferred_element_type=F32)

    def set_max(h, value):
        high, low = split(value)
        m_refs[h][...] = high.astype(F32) + low.astype(F32)
        qa_ref[h, size : size + 16, :] = jnp.concatenate(
            [-high, -low, jnp.zeros((14, latents), BF16)], axis=0
        )

    for h in range(heads):
        if first:
            set_max(h, jnp.max(scores(h, pl.ds(0, 128)), axis=0, keepdims=True))
        else:
            set_max(h, m_ins[h][...])

    def add(h, keys):
        probs = jnp.exp2(scores(h, keys)).astype(BF16)
        return lax.dot_general(v_ref[h, :, keys], probs, PLAIN, preferred_element_type=F32)

    for h in range(heads):
        acc_ref, m_ref = acc_refs[h], m_refs[h]
        for t in range(0, tokens, BLOCK):
            more = add(h, pl.ds(t, min(BLOCK, tokens - t)))
            if t > 0:
                acc_ref[...] += more
            else:
                acc_ref[...] = more if first else acc_ins[h][...] + more

        @pl.when(jnp.logical_not(jnp.max(acc_ref[size : size + 8, :]) < LIMIT))
        def _(h=h, acc_ref=acc_ref, m_ref=m_ref):
            before = m_ref[...]
            qa_ref[h, size:, :] = jnp.zeros((size, latents), BF16)

            def at(t):
                return pl.ds(pl.multiple_of(t * block, block), block)

            def widen(t, best):
                return jnp.maximum(best, jnp.max(scores(h, at(t)), axis=0, keepdims=True))

            set_max(h, lax.fori_loop(0, steps, widen, before))
            if first:
                acc_ref[...] = jnp.zeros((ROWS, latents), F32)
            else:
                acc_ref[...] = acc_ins[h][...] * jnp.exp2(before - m_ref[...])

            def redo(t, carry):
                acc_ref[...] += add(h, at(t))
                return carry

            lax.fori_loop(0, steps, redo, 0)

        if not first:
            for i in range(latents // 128):
                lanes = pl.ds(128 * i, 128)
                acc, total, m = acc_ref[:size, lanes], acc_ref[size : size + 1, lanes], m_ref[:, lanes]
                for side in range(2):
                    pay_refs[h][2 * i + side] = pack(fold_half(acc, side), both(total, side), both(m, side))


def both(row, side):
    lane = lax.broadcasted_iota(jnp.int32, row.shape, 1)
    keep = lane < 64 if side == 0 else lane >= 64
    return jnp.where(keep, row, pltpu.roll(row, 64, 1))


def fold_half(acc, side):
    half = acc.shape[0] // 2
    low, high = acc[:half], acc[half:]
    if side == 0:
        high = pltpu.roll(high, 64, 1)
    else:
        low = pltpu.roll(low, 64, 1)
    lane = lax.broadcasted_iota(jnp.int32, low.shape, 1)
    return jnp.where(lane < 64, low, high)


def pack(acc, total, m):
    t_high, m_high = total.astype(BF16).astype(F32), m.astype(BF16).astype(F32)
    fill = jnp.zeros((PAY - acc.shape[0] - 4, acc.shape[1]), F32)
    rows = [acc, t_high, total - t_high, m_high, m - m_high, fill]
    return jnp.concatenate(rows, axis=0).astype(BF16)


def attend(x, rstd, w, b, q, at=None, state=()):
    heads, size, latents = q.shape
    first = at is None
    vmem = pl.BlockSpec(memory_space=pltpu.VMEM)
    tokens = rstd.shape[0]
    accs = [jax.ShapeDtypeStruct((ROWS, latents), F32)] * heads
    ms = [jax.ShapeDtypeStruct((1, latents), F32)] * heads
    scratch = [
        pltpu.VMEM((heads, 2 * size, latents), BF16),
        pltpu.VMEM((heads, tokens, 2 * size), BF16),
        pltpu.VMEM((heads, ROWS, tokens), BF16),
    ]
    if first:
        ins, in_specs, out = (x, rstd, w, b, q), [vmem] * 5, accs + ms
    else:
        count = x.shape[0] - tokens
        ins = (at, x, rstd, w, b, q, *state)
        in_specs = [pl.BlockSpec(memory_space=pltpu.SMEM), pl.BlockSpec(memory_space=pl.ANY)]
        in_specs += [vmem] * (len(ins) - 2)
        out = [jax.ShapeDtypeStruct((latents // 64, PAY, 128), BF16)] * heads
        scratch = [pltpu.VMEM(i.shape, F32) for i in accs + ms] + scratch
        scratch += [
            pltpu.VMEM((tokens // count, count, x.shape[1]), BF16),
            pltpu.SemaphoreType.DMA((tokens // count,)),
        ]
    work = tokens * latents * heads
    return pl.pallas_call(
        functools.partial(attend_kernel, first),
        out_shape=out,
        in_specs=in_specs,
        out_specs=[vmem] * len(out),
        scratch_shapes=scratch,
        compiler_params=pltpu.CompilerParams(vmem_limit_bytes=56 << 20),
        cost_estimate=pl.CostEstimate(
            flops=16 * work * size, bytes_accessed=tokens * 1536, transcendentals=work
        ),
        name="attend",
    )(*ins)


def merge(parts):
    half = 32
    ms = [p[half + 2 : half + 3] + p[half + 3 : half + 4] for p in parts]
    top = functools.reduce(jnp.maximum, ms)
    acc, total = 0.0, 0.0
    for p, m in zip(parts, ms):
        factor = jnp.exp2(m - top)
        acc = acc + p[:half] * factor
        total = total + (p[half : half + 1] + p[half + 1 : half + 2]) * factor
    return acc, total, top


def combine_kernel(one_ref, two_ref, out_ref):
    for j in range(one_ref.shape[0]):
        out_ref[j] = pack(*merge([one_ref[j].astype(F32), two_ref[j].astype(F32)]))


def finish_kernel(parts_ref, out_ref):
    acc, total, _ = merge([parts_ref[i].astype(F32) for i in range(parts_ref.shape[0])])
    result = (acc / total).astype(BF16)
    for i in range(out_ref.shape[0]):
        out_ref[i] = result


def combine(one, two):
    vmem = pl.BlockSpec(memory_space=pltpu.VMEM)
    return pl.pallas_call(
        combine_kernel,
        out_shape=jax.ShapeDtypeStruct(one.shape, BF16),
        in_specs=[vmem] * 2,
        out_specs=vmem,
        name="combine",
    )(one, two)


def finish(parts, copies):
    vmem = pl.BlockSpec(memory_space=pltpu.VMEM)
    return pl.pallas_call(
        finish_kernel,
        out_shape=jax.ShapeDtypeStruct((copies, 32, 128), BF16),
        in_specs=[vmem],
        out_specs=vmem,
        name="finish",
    )(parts)


def place_kernel(parts_ref, out_ref):
    half = parts_ref.shape[1]
    for i in range(parts_ref.shape[0] // 2):
        one, two = parts_ref[2 * i].astype(F32), parts_ref[2 * i + 1].astype(F32)
        lane = lax.broadcasted_iota(jnp.int32, one.shape, 1)
        low = jnp.where(lane < 64, one, pltpu.roll(two, 64, 1))
        high = jnp.where(lane < 64, pltpu.roll(one, 64, 1), two)
        out_ref[:half, pl.ds(128 * i, 128)] = low.astype(BF16)
        out_ref[half:, pl.ds(128 * i, 128)] = high.astype(BF16)


def place(parts):
    vmem = pl.BlockSpec(memory_space=pltpu.VMEM)
    return pl.pallas_call(
        place_kernel,
        out_shape=jax.ShapeDtypeStruct((64, 64 * parts.shape[0]), BF16),
        in_specs=[vmem],
        out_specs=vmem,
        name="place",
    )(parts)


def exchange(parts, axis):
    return lax.all_to_all(parts, axis, split_axis=0, concat_axis=0, tiled=True)


def shift(block, axis, by):
    size = lax.axis_size(axis)
    return lax.ppermute(block, axis, [(i, (i + by) % size) for i in range(size)])


def body(patches, w_patch, patch_bias, w_kv, queries):
    size = queries.shape[1]
    tokens = patches.shape[0]
    gathered = lax.all_gather(patches, "z", axis=0, tiled=True)

    weight = w_patch.astype(F32)
    weight = weight - jnp.mean(weight, axis=1, keepdims=True)
    bias = patch_bias - jnp.mean(patch_bias)
    embed = jnp.dot(patches, w_patch, preferred_element_type=F32) + patch_bias
    mean = jnp.mean(embed, axis=-1, keepdims=True)
    var = jnp.mean((embed - mean) * (embed - mean), axis=-1)
    rstd = lax.rsqrt(var + 1e-05)
    mine = rstd.reshape(-1, 1)
    rstd = exchange(jnp.broadcast_to(rstd[None], (lax.axis_size("z"), tokens)), "z")
    at = lax.axis_index("z")
    turned = lax.dynamic_slice_in_dim(jnp.concatenate([rstd, rstd]), at + 1, rstd.shape[0] - 1, axis=0)

    w_pair = jnp.stack([shift(w_kv, "c", 1), w_kv])
    q_pair = jnp.stack([shift(queries.T, "c", 1), queries.T])
    scale = jnp.where(jnp.arange(2 * size) < size, LOG2E * float(size) ** (-0.5), 1.0)
    fold = jnp.einsum("pd,hdn->hpn", weight, w_pair.astype(F32), precision=lax.Precision.HIGHEST)
    fold = (fold * scale).astype(BF16)
    fold_bias = jnp.einsum("d,hdn->hn", bias, w_pair.astype(F32), precision=lax.Precision.HIGHEST)
    fold_bias = fold_bias * scale

    weights = (jnp.concatenate([fold[0], fold[1]], axis=1), fold_bias.reshape(1, -1), q_pair)
    state = attend(patches, mine, *weights)
    other, own = attend(gathered, turned.reshape(-1, 1), *weights, at.reshape(1), state)

    with jax.named_scope("totals"):
        part = exchange(combine(own, shift(other, "c", 1)), ("y", "x"))
        part = finish(part, part.shape[0])
    with jax.named_scope("readout"):
        return place(exchange(part, ("y", "x"))).T


def solution(mesh):
    grid = Mesh(mesh.devices.reshape(8, 4, 8, 2), ("y", "x", "z", "c"))
    head = P(None, ("z", "c"))
    placed = (P(("y", "x", "z", "c"), None), P(), P(), head, head)
    return jax.shard_map(body, mesh=grid, in_specs=placed, out_specs=head, check_vma=False)
```

```python
import functools

import jax
import jax.numpy as jnp
from jax import lax
from jax.experimental import pallas as pl
from jax.experimental.pallas import tpu as pltpu
from jax.sharding import Mesh
from jax.sharding import PartitionSpec as P

F32 = jnp.float32
BF16 = jnp.bfloat16
LOG2E = 1.4426950408889634
LIMIT = 2.0**64
ROWS = 80
BLOCK = 1024
PAY = 40
PLAIN = (((1,), (0,)), ((), ()))


def split(value):
    high = value.astype(BF16)
    return high, (value - high.astype(F32)).astype(BF16)


def attend_kernel(first, *refs):
    if first:
        x_ref, rstd_ref, w_ref, b_ref, q_ref, *refs = refs
        acc_refs, m_refs, (qa_ref, k_ref, v_ref) = refs[:2], refs[2:4], refs[4:]
    else:
        at_ref, x_ref, rstd_ref, w_ref, b_ref, q_ref, *refs = refs
        acc_ins, m_ins, pay_refs, refs = refs[:2], refs[2:4], refs[4:6], refs[6:]
        acc_refs, m_refs, (qa_ref, k_ref, v_ref, x_buf, sems, acc_bufs, acc_sems) = refs[:2], refs[2:4], refs[4:]
    tokens = k_ref.shape[1]
    heads, size, latents = q_ref.shape
    block = 128
    steps = tokens // block

    if not first:
        pieces, count = x_buf.shape[:2]
        copies = []
        for t in range(pieces):
            place = lax.rem(at_ref[0] + t + 1, pieces + 1)
            rows = pl.ds(pl.multiple_of(place * count, count), count)
            copies.append(pltpu.make_async_copy(x_ref.at[rows], x_buf.at[t], sems.at[t]))
            copies[t].start()
        sums = [pltpu.make_async_copy(acc_ins[h], acc_bufs.at[h], acc_sems.at[h]) for h in range(heads)]
        for copy in sums:
            copy.start()

    def project(x, start, count):
        kv = jnp.dot(x, w_ref[...], preferred_element_type=F32)
        rows = [rstd_ref[i : i + 1, :] for i in range(start // 128, (start + count) // 128)]
        scale = jnp.concatenate([jnp.broadcast_to(row, (128, 128)).T for row in rows], axis=0)
        kv = kv + b_ref[...]
        lane = lax.broadcasted_iota(jnp.int32, (count, 2 * size), 1)
        for h in range(heads):
            mine = (kv[:, 2 * size * h : 2 * size * (h + 1)] * scale).astype(BF16)
            k_ref[h, pl.ds(start, count), :] = jnp.where(lane < size, mine, jnp.ones_like(mine))
            v_ref[h, :size, pl.ds(start, count)] = mine.T[size:, :]

    for h in range(heads):
        v_ref[h, size:, :] = jnp.ones((ROWS - size, tokens), BF16)
        qa_ref[h, :size, :] = q_ref[h]
        qa_ref[h, size:, :] = jnp.zeros((size, latents), BF16)

    if first:
        project(x_ref[...], 0, tokens)
    else:
        for t in range(pieces):
            copies[t].wait()
            project(x_buf[t], t * count, count)

    def scores(h, keys):
        return lax.dot_general(k_ref[h, keys, :], qa_ref[h], PLAIN, preferred_element_type=F32)

    def set_max(h, value):
        high, low = split(value)
        m_refs[h][...] = high.astype(F32) + low.astype(F32)
        qa_ref[h, size : size + 16, :] = jnp.concatenate(
            [-high, -low, jnp.zeros((14, latents), BF16)], axis=0
        )

    for h in range(heads):
        if first:
            set_max(h, jnp.max(scores(h, pl.ds(0, 128)), axis=0, keepdims=True))
        else:
            set_max(h, m_ins[h][...])

    def add(h, keys):
        probs = jnp.exp2(scores(h, keys)).astype(BF16)
        return lax.dot_general(v_ref[h, :, keys], probs, PLAIN, preferred_element_type=F32)

    for h in range(heads):
        acc_ref, m_ref = acc_refs[h], m_refs[h]
        if not first:
            sums[h].wait()
        for t in range(0, tokens, BLOCK):
            more = add(h, pl.ds(t, min(BLOCK, tokens - t)))
            if t > 0:
                acc_ref[...] += more
            else:
                acc_ref[...] = more if first else acc_bufs[h] + more

        @pl.when(jnp.logical_not(jnp.max(acc_ref[size : size + 8, :]) < LIMIT))
        def _(h=h, acc_ref=acc_ref, m_ref=m_ref):
            before = m_ref[...]
            qa_ref[h, size:, :] = jnp.zeros((size, latents), BF16)

            def at(t):
                return pl.ds(pl.multiple_of(t * block, block), block)

            def widen(t, best):
                return jnp.maximum(best, jnp.max(scores(h, at(t)), axis=0, keepdims=True))

            set_max(h, lax.fori_loop(0, steps, widen, before))
            if first:
                acc_ref[...] = jnp.zeros((ROWS, latents), F32)
            else:
                acc_ref[...] = acc_bufs[h] * jnp.exp2(before - m_ref[...])

            def redo(t, carry):
                acc_ref[...] += add(h, at(t))
                return carry

            lax.fori_loop(0, steps, redo, 0)

        if not first:
            for i in range(latents // 128):
                lanes = pl.ds(128 * i, 128)
                acc, total, m = acc_ref[:size, lanes], acc_ref[size : size + 1, lanes], m_ref[:, lanes]
                for side in range(2):
                    pay_refs[h][2 * i + side] = pack(fold_half(acc, side), both(total, side), both(m, side))


def both(row, side):
    lane = lax.broadcasted_iota(jnp.int32, row.shape, 1)
    keep = lane < 64 if side == 0 else lane >= 64
    return jnp.where(keep, row, pltpu.roll(row, 64, 1))


def fold_half(acc, side):
    half = acc.shape[0] // 2
    low, high = acc[:half], acc[half:]
    if side == 0:
        high = pltpu.roll(high, 64, 1)
    else:
        low = pltpu.roll(low, 64, 1)
    lane = lax.broadcasted_iota(jnp.int32, low.shape, 1)
    return jnp.where(lane < 64, low, high)


def pack(acc, total, m):
    t_high, m_high = total.astype(BF16).astype(F32), m.astype(BF16).astype(F32)
    fill = jnp.zeros((PAY - acc.shape[0] - 4, acc.shape[1]), F32)
    rows = [acc, t_high, total - t_high, m_high, m - m_high, fill]
    return jnp.concatenate(rows, axis=0).astype(BF16)


def attend(x, rstd, w, b, q, at=None, state=()):
    heads, size, latents = q.shape
    first = at is None
    vmem = pl.BlockSpec(memory_space=pltpu.VMEM)
    tokens = rstd.size
    accs = [jax.ShapeDtypeStruct((ROWS, latents), F32)] * heads
    ms = [jax.ShapeDtypeStruct((1, latents), F32)] * heads
    scratch = [
        pltpu.VMEM((heads, 2 * size, latents), BF16),
        pltpu.VMEM((heads, tokens, 2 * size), BF16),
        pltpu.VMEM((heads, ROWS, tokens), BF16),
    ]
    if first:
        ins, in_specs, out = (x, rstd, w, b, q), [vmem] * 5, accs + ms
    else:
        count = x.shape[0] - tokens
        ins = (at, x, rstd, w, b, q, *state)
        in_specs = [pl.BlockSpec(memory_space=pltpu.SMEM), pl.BlockSpec(memory_space=pl.ANY)]
        in_specs += [vmem] * 4 + [pl.BlockSpec(memory_space=pl.ANY)] * heads + [vmem] * heads
        out = [jax.ShapeDtypeStruct((latents // 64, PAY, 128), BF16)] * heads
        scratch = [pltpu.VMEM(i.shape, F32) for i in accs + ms] + scratch
        scratch += [
            pltpu.VMEM((tokens // count, count, x.shape[1]), BF16),
            pltpu.SemaphoreType.DMA((tokens // count,)),
            pltpu.VMEM((heads, ROWS, latents), F32),
            pltpu.SemaphoreType.DMA((heads,)),
        ]
    work = tokens * latents * heads
    return pl.pallas_call(
        functools.partial(attend_kernel, first),
        out_shape=out,
        in_specs=in_specs,
        out_specs=[vmem] * len(out),
        scratch_shapes=scratch,
        compiler_params=pltpu.CompilerParams(vmem_limit_bytes=56 << 20),
        cost_estimate=pl.CostEstimate(
            flops=16 * work * size, bytes_accessed=tokens * 1536, transcendentals=work
        ),
        name="attend",
    )(*ins)


def merge(parts):
    half = 32
    ms = [p[half + 2 : half + 3] + p[half + 3 : half + 4] for p in parts]
    top = functools.reduce(jnp.maximum, ms)
    acc, total = 0.0, 0.0
    for p, m in zip(parts, ms):
        factor = jnp.exp2(m - top)
        acc = acc + p[:half] * factor
        total = total + (p[half : half + 1] + p[half + 1 : half + 2]) * factor
    return acc, total, top


def combine_kernel(one_ref, two_ref, out_ref):
    for j in range(one_ref.shape[0]):
        out_ref[j] = pack(*merge([one_ref[j].astype(F32), two_ref[j].astype(F32)]))


def finish_kernel(parts_ref, out_ref):
    acc, total, _ = merge([parts_ref[i].astype(F32) for i in range(parts_ref.shape[0])])
    result = (acc / total).astype(BF16)
    for i in range(out_ref.shape[0]):
        out_ref[i] = result


def combine(one, two):
    vmem = pl.BlockSpec(memory_space=pltpu.VMEM)
    return pl.pallas_call(
        combine_kernel,
        out_shape=jax.ShapeDtypeStruct(one.shape, BF16),
        in_specs=[vmem] * 2,
        out_specs=vmem,
        name="combine",
    )(one, two)


def finish(parts, copies):
    vmem = pl.BlockSpec(memory_space=pltpu.VMEM)
    return pl.pallas_call(
        finish_kernel,
        out_shape=jax.ShapeDtypeStruct((copies, 32, 128), BF16),
        in_specs=[vmem],
        out_specs=vmem,
        name="finish",
    )(parts)


def place_kernel(parts_ref, out_ref):
    half = parts_ref.shape[1]
    for i in range(parts_ref.shape[0] // 2):
        one, two = parts_ref[2 * i].astype(F32), parts_ref[2 * i + 1].astype(F32)
        lane = lax.broadcasted_iota(jnp.int32, one.shape, 1)
        low = jnp.where(lane < 64, one, pltpu.roll(two, 64, 1))
        high = jnp.where(lane < 64, pltpu.roll(one, 64, 1), two)
        out_ref[:half, pl.ds(128 * i, 128)] = low.astype(BF16)
        out_ref[half:, pl.ds(128 * i, 128)] = high.astype(BF16)


def place(parts):
    vmem = pl.BlockSpec(memory_space=pltpu.VMEM)
    return pl.pallas_call(
        place_kernel,
        out_shape=jax.ShapeDtypeStruct((64, 64 * parts.shape[0]), BF16),
        in_specs=[vmem],
        out_specs=vmem,
        name="place",
    )(parts)


def exchange(parts, axis):
    return lax.all_to_all(parts, axis, split_axis=0, concat_axis=0, tiled=True)


def shift(block, axis, by):
    size = lax.axis_size(axis)
    return lax.ppermute(block, axis, [(i, (i + by) % size) for i in range(size)])


def body(patches, w_patch, patch_bias, w_kv, queries):
    size = queries.shape[1]
    tokens = patches.shape[0]
    gathered = lax.all_gather(patches, "z", axis=0, tiled=True)

    weight = w_patch.astype(F32)
    weight = weight - jnp.mean(weight, axis=1, keepdims=True)
    bias = patch_bias - jnp.mean(patch_bias)
    embed = jnp.dot(patches, w_patch, preferred_element_type=F32) + patch_bias
    mean = jnp.mean(embed, axis=-1, keepdims=True)
    var = jnp.mean((embed - mean) * (embed - mean), axis=-1)
    rstd = lax.rsqrt(var + 1e-05)
    mine = rstd.reshape(-1, 128)
    rstd = exchange(jnp.broadcast_to(rstd[None], (lax.axis_size("z"), tokens)), "z")
    at = lax.axis_index("z")
    turned = lax.dynamic_slice_in_dim(jnp.concatenate([rstd, rstd]), at + 1, rstd.shape[0] - 1, axis=0)

    w_pair = jnp.stack([shift(w_kv, "c", 1), w_kv])
    q_pair = jnp.stack([shift(queries.T, "c", 1), queries.T])
    scale = jnp.where(jnp.arange(2 * size) < size, LOG2E * float(size) ** (-0.5), 1.0)
    fold = jnp.einsum("pd,hdn->hpn", weight, w_pair.astype(F32), precision=lax.Precision.HIGHEST)
    fold = (fold * scale).astype(BF16)
    fold_bias = jnp.einsum("d,hdn->hn", bias, w_pair.astype(F32), precision=lax.Precision.HIGHEST)
    fold_bias = fold_bias * scale

    weights = (jnp.concatenate([fold[0], fold[1]], axis=1), fold_bias.reshape(1, -1), q_pair)
    state = attend(patches, mine, *weights)
    other, own = attend(gathered, turned.reshape(-1, 128), *weights, at.reshape(1), state)

    with jax.named_scope("totals"):
        part = exchange(combine(own, shift(other, "c", 1)), ("y", "x"))
        part = finish(part, part.shape[0])
    with jax.named_scope("readout"):
        return place(exchange(part, ("y", "x"))).T


def solution(mesh):
    grid = Mesh(mesh.devices.reshape(8, 4, 8, 2), ("y", "x", "z", "c"))
    head = P(None, ("z", "c"))
    placed = (P(("y", "x", "z", "c"), None), P(), P(), head, head)
    return jax.shard_map(body, mesh=grid, in_specs=placed, out_specs=head, check_vma=False)
```
